32 devices in a mesh: row: 4 (over y, x), col: 8 (over z, core).
Axes of the slice: x: 2, y: 2, z: 4, core: 2. Of those that a mesh axis runs over, the one named last changes fastest.
Arguments:
- schur: float32 [8192, 8192], P('row', 'col'), may hold values from -6 to 6
- panel_raw: bfloat16 [8192, 1024], P('col', 'row'), may hold values from -0.59765625 to 0.59765625
- diag_inverse: bfloat16 [1024, 1024], replicated, may hold values from -1 to 2, as said below
- perm: int32 [64], replicated, may hold values from 0 to 63, as said below
- pattern: int32 [64, 64], P('row', 'col'), may hold values 0 or 1
Outputs:
- schur_out: float32 [8192, 8192], P('row', 'col')
The draws below stay inside these ranges and needn't reach their ends.
Inputs may be any that keep to these rules, and one draw needn't show every extreme that they name: diag_inverse is lower triangular with diagonal entries between 0.5 and 2. perm names every block row once. Holder h holds the owner-order blocks h * 8 to (h + 1) * 8 - 1; a column group is a run of 8 consecutive global block rows starting at a multiple of it. The blocks of one holder fall into the column groups as evenly as possible: at most 1 into one group, and exactly 1 into some group.
All inputs are finite; a program needn't handle non-finite values. No bound on the sum of `pattern` on one device may be relied on, other than what follows from the above.
Results may differ from the reference program's by a relative error of at most 0.007.
Values may be sent and summed in bfloat16 or wider, within the bound.
A program may use at most 192 MiB of HBM per device.

```python
import jax
import jax.numpy as jnp
from jax import lax

BLK = 128
SNW = 1024
NB = 64
OWNERS = 8


def draw_diag_inverse(key, part):
    key_off = jax.random.fold_in(key, 11)
    key_diag = jax.random.fold_in(key, 12)
    indices = jnp.arange(SNW, dtype=jnp.int32)
    below = indices[:, None] > indices[None, :]
    on_diag = indices[:, None] == indices[None, :]
    spread = 0.5 / jnp.sqrt(jnp.float32(SNW))
    off_part = jax.random.truncated_normal(key_off, -3.0, 3.0, (SNW, SNW), jnp.float32) * spread
    diag_part = jnp.exp(jax.random.uniform(key_diag, (SNW,), jnp.float32, -0.69, 0.69))
    result = jnp.where(below, off_part, 0.0) + jnp.where(on_diag, diag_part[None, :], 0.0)
    return result.astype(jnp.bfloat16)


def shuffle_rows(base_key, count, length):
    subkeys = jax.random.split(base_key, count)
    return jax.vmap(lambda subkey: jax.random.permutation(subkey, length))(subkeys)


def draw_perm(key, part):
    own_count = NB // OWNERS
    key_offsets = jax.random.fold_in(key, 21)
    key_labels = jax.random.fold_in(key, 22)
    key_within = jax.random.fold_in(key, 23)
    key_orders = jax.random.fold_in(key, 24)
    offsets = jax.random.permutation(key_offsets, OWNERS)
    labels = jax.random.permutation(key_labels, OWNERS)
    step_ids = jnp.arange(own_count, dtype=jnp.int32)
    groups = labels[(offsets[:, None] + step_ids[None, :]) % OWNERS]
    within = shuffle_rows(key_within, OWNERS, own_count)
    target = groups * own_count + within[groups, step_ids[None, :]]
    orders = shuffle_rows(key_orders, OWNERS, own_count)
    return jnp.take_along_axis(target, orders, axis=1).reshape(NB).astype(jnp.int32)


def plant(array, own_key, low, largest):
    index_at = [jax.random.randint(jax.random.fold_in(own_key, axis), (), 0, length) for axis, length in enumerate(array.shape)]
    longest = array.shape.index(max(array.shape))
    neighbour = index_at[:longest] + [(index_at[longest] + 1) % array.shape[longest]] + index_at[longest + 1:]
    return array.at[tuple(index_at)].set(low).at[tuple(neighbour)].set(largest)


def block_scale(key, extent, shards, low, top_value):
    def one(dim, blocks):
        steps = jax.random.uniform(jax.random.fold_in(jax.random.fold_in(key, 6), dim), (blocks,), jnp.float32, low / len(shards), top_value / len(shards))
        return jnp.repeat(jnp.exp(steps), extent[dim] // blocks).reshape((-1,) + (1,) * (len(extent) - dim - 1))

    factor_of = one(*shards[0])
    for cut in shards[1:]:
        factor_of = factor_of * one(*cut)
    return factor_of


def gaussian(key, shape, deviation, limit, cuts=(), held_as=jnp.bfloat16):
    loudness = block_scale(key, shape, cuts, -0.22, 0.18) if cuts else 1.0
    entries = jax.random.normal(key, shape, jnp.float32) * deviation * loudness
    return jnp.minimum(jnp.maximum(entries, -limit), limit).astype(held_as)


def setup_inputs(seed: int = 0) -> dict:
    key_list = jax.random.split(jax.random.key(seed), 6)
    return {
        "schur": gaussian(key_list[0], (NB * BLK, NB * BLK), 1.0, 6.0, ((0, 4), (1, 8)), jnp.float32),
        "panel_raw": gaussian(key_list[1], (NB * BLK, SNW), 0.1, 0.59765625, ((0, 8), (1, 4))),
        "diag_inverse": draw_diag_inverse(jax.random.fold_in(key_list[5], 71), 0),
        "perm": draw_perm(jax.random.fold_in(key_list[5], 71), 0),
        "pattern": plant((jax.random.randint(key_list[4], (NB, NB), 0, 2) < 1).astype(jnp.int32), jax.random.fold_in(key_list[4], 1), 0, 1),
    }


def reference(schur, panel_raw, diag_inverse, perm, pattern):
    owned = lax.dot_general(panel_raw, diag_inverse, (((1,), (1,)), ((), ())), preferred_element_type=jnp.float32).astype(jnp.bfloat16)
    position = jnp.zeros((NB,), jnp.int32).at[perm].set(jnp.arange(NB, dtype=jnp.int32))
    panel = owned.reshape(NB, BLK, SNW)[position].reshape(NB * BLK, SNW)

    def one_row(inputs):
        rows_now, mask_row, panel_row = inputs
        update = lax.dot_general(panel_row, panel, (((1,), (1,)), ((), ())), preferred_element_type=jnp.float32)
        weight = jnp.repeat(mask_row.astype(jnp.float32), BLK, total_repeat_length=NB * BLK)
        return rows_now - update * weight[None, :]

    result = lax.map(one_row, (schur.reshape(NB, BLK, NB * BLK), pattern, panel.reshape(NB, BLK, SNW)))
    return result.reshape(NB * BLK, NB * BLK)
```

```python
import functools

import jax
import jax.numpy as jnp
from jax import lax
from jax.experimental import pallas as pl
from jax.experimental.pallas import tpu as pltpu
from jax.sharding import PartitionSpec as P

BLK = 128
MESH = pl.DeviceIdType.MESH


def times_inverse(left, right):
    return lax.dot_general(
        left, right, (((1,), (1,)), ((), ())), preferred_element_type=jnp.float32
    )


def general_exchange(
    n_row, n_col, gpr, held, block_cols, block_rows,
    perm_ref, raw_hbm, d_hbm, rows_ref, cols_hbm, table_ref,
    raw_ref, sorted_ref, a_ref, b_ref, own_ref, d_ref, cpan_ref, cols_ref,
    a_send, a_recv, b_send, b_recv, c_send, c_recv,
    up_send, up_recv, down_send, down_recv, f_send, f_recv, loc,
):
    r = lax.axis_index("row")
    c = lax.axis_index("col")
    n_pos = n_col // 2
    pos = c // 2
    core = c % 2
    sibling = pos * 2 + (1 - core)
    kw = raw_ref.shape[2]
    snw = d_ref.shape[0]
    load_raw = pltpu.make_async_copy(raw_hbm, raw_ref, loc.at[3])
    load_raw.start()
    load_d = pltpu.make_async_copy(d_hbm, d_ref, loc.at[0])
    load_d.start()

    def remote(src, dst, ssem, rsem, rr, cc):
        return pltpu.make_async_remote_copy(
            src_ref=src, dst_ref=dst, send_sem=ssem, recv_sem=rsem,
            device_id=(rr, cc), device_id_type=MESH,
        )

    def part(index):
        return pl.ds(pl.multiple_of(index * kw, kw), kw)

    barrier = pltpu.get_barrier_semaphore()
    for dr in range(1, n_row):
        pl.semaphore_signal(barrier, inc=1, device_id=((r + dr) % n_row, c), device_id_type=MESH)
    for dc in range(1, n_col):
        pl.semaphore_signal(barrier, inc=1, device_id=(r, (c + dc) % n_col), device_id_type=MESH)
    groups = [lax.div(perm_ref[c * held + i], block_cols) for i in range(held)]
    load_raw.wait()
    for g in range(n_col):
        block = 0
        for i in range(1, held):
            block = jnp.where(groups[i] == g, i, block)
        sorted_ref[g] = raw_ref[block]
    pl.semaphore_wait(barrier, n_row + n_col - 2)

    def a_copy(dr, q, came=None):
        to = (r + dr) % n_row
        return remote(sorted_ref.at[to * gpr + q],
                      a_ref.at[q, :, part(r if came is None else came)],
                      a_send.at[dr, q], a_recv.at[dr, q], to, c)

    def b_copy(dc, came=None):
        to = (c + dc) % n_col
        return remote(sorted_ref.at[to], b_ref.at[c if came is None else came],
                      b_send.at[dc], b_recv.at[dc], r, to)

    for q in range(gpr):
        for dr in range(1, n_row):
            a_copy(dr, q).start()
    for dc in range(1, n_col):
        b_copy(dc).start()
    a_ref[:, :, part(r)] = sorted_ref[pl.ds(r * gpr, gpr)]
    b_ref[c] = sorted_ref[c]
    load_d.wait()
    def up_copy(d, q):
        slot = (pos - d) * 2 + core
        return remote(own_ref.at[q] if d == 0 else rows_ref.at[slot, q], rows_ref.at[slot, q],
                      up_send.at[d, q], up_recv.at[d, q], r, (pos + 1) * 2 + core)

    def down_copy(d, q):
        slot = (pos + d) * 2 + core
        return remote(own_ref.at[q] if d == 0 else rows_ref.at[slot, q], rows_ref.at[slot, q],
                      down_send.at[d, q], down_recv.at[d, q], r, (pos - 1) * 2 + core)

    def side_copy(source, q, mine):
        slot = source * 2 + core
        return remote(own_ref.at[q] if mine else rows_ref.at[slot, q], rows_ref.at[slot, q],
                      f_send.at[source, q], f_recv.at[source, q], r, sibling)

    for q in range(gpr):
        for dr in range(1, n_row):
            a_copy(dr, q, (r + n_row - dr) % n_row).wait_recv()
        own_ref[q] = times_inverse(a_ref[q], d_ref[...]).astype(jnp.bfloat16)

        @pl.when(pos < n_pos - 1)
        def _(q=q):
            up_copy(0, q).start()

        @pl.when(pos > 0)
        def _(q=q):
            down_copy(0, q).start()

    for q in range(gpr):
        side_copy(pos, q, True).start()
    keep = pltpu.make_async_copy(own_ref, rows_ref.at[c], loc.at[1])
    keep.start()

    for dc in range(1, n_col):
        b_copy(dc, (c + n_col - dc) % n_col).wait_recv()

    def c_copy(dr, came=None):
        return remote(b_ref, cpan_ref.at[:, :, part(r if came is None else came)],
                      c_send.at[dr], c_recv.at[dr], (r + dr) % n_row, c)

    for dr in range(1, n_row):
        c_copy(dr).start()
    cpan_ref[:, :, part(r)] = b_ref[...]

    wanted = [c * block_cols + k for k in range(block_cols)]
    wanted += [r * block_rows + k for k in range(block_rows)]

    def look(p, found):
        at, holder = perm_ref[p], p // held
        return tuple(jnp.where(at == w, holder, f) for w, f in zip(wanted, found))

    holders = lax.fori_loop(
        0, perm_ref.shape[0], look, tuple(jnp.int32(0) for _ in wanted)
    )
    for k, value in enumerate(holders):
        table_ref[k] = value

    keep_cols = pltpu.make_async_copy(cols_ref, cols_hbm, loc.at[2])

    def factor_columns():
        for dr in range(1, n_row):
            c_copy(dr, (r + n_row - dr) % n_row).wait_recv()
        step = 4 if block_cols % 4 == 0 else 1
        for w in range(0, block_cols, step):
            left = jnp.concatenate([cpan_ref[holders[w + k]] for k in range(step)], axis=0)
            done = times_inverse(left, d_ref[...]).astype(jnp.bfloat16)
            cols_ref[w * BLK:(w + step) * BLK, :] = done
        keep_cols.start()

    for d in range(1, n_pos):
        if d == n_pos - 1:
            factor_columns()

        for q in range(gpr):
            @pl.when(pos - d >= 0)
            def _(d=d, q=q):
                slot = (pos - d) * 2 + core
                remote(own_ref.at[q], rows_ref.at[slot, q], up_send.at[d - 1, q],
                       up_recv.at[d - 1, q], r, sibling).wait_recv()
                if d < n_pos - 1:
                    @pl.when(pos < n_pos - 1)
                    def _():
                        up_copy(d, q).start()
                side_copy(pos - d, q, False).start()

            @pl.when(pos + d <= n_pos - 1)
            def _(d=d, q=q):
                slot = (pos + d) * 2 + core
                remote(own_ref.at[q], rows_ref.at[slot, q], down_send.at[d - 1, q],
                       down_recv.at[d - 1, q], r, sibling).wait_recv()
                if d < n_pos - 1:
                    @pl.when(pos > 0)
                    def _():
                        down_copy(d, q).start()
                side_copy(pos + d, q, False).start()

    for dr in range(1, n_row):
        for q in range(gpr):
            a_copy(dr, q).wait_send()
        c_copy(dr).wait_send()
    for dc in range(1, n_col):
        b_copy(dc).wait_send()
    for q in range(gpr):
        for d in range(n_pos - 1):
            @pl.when((pos - d >= 0) & (pos < n_pos - 1))
            def _(d=d, q=q):
                up_copy(d, q).wait_send()

            @pl.when((pos + d <= n_pos - 1) & (pos > 0))
            def _(d=d, q=q):
                down_copy(d, q).wait_send()
        for source in range(n_pos):
            slot = source * 2 + (1 - core)
            remote(own_ref.at[q], rows_ref.at[slot, q], f_send.at[source, q],
                   f_recv.at[source, q], r, sibling).wait_recv()
            side_copy(source, q, True).wait_send()
    keep.wait()
    keep_cols.wait()


def general_update(tile, table, pat_ref, *refs):
    row_refs, (cols_ref, schur_ref, out_ref) = refs[:tile], refs[tile:]
    i = pl.program_id(0)
    left = jnp.concatenate([ref[0, 0] for ref in row_refs], axis=0)
    update = times_inverse(left, cols_ref[...])
    for e in range(tile):
        rows = slice(e * BLK, (e + 1) * BLK)
        for w in range(cols_ref.shape[0] // BLK):
            at = slice(w * BLK, (w + 1) * BLK)
            weight = pat_ref[w, tile * i + e].astype(jnp.float32)
            out_ref[rows, at] = schur_ref[rows, at] - update[rows, at] * weight


def general_local(schur, panel_raw, diag_inverse, perm, pattern):
    n_row = lax.axis_size("row")
    n_col = lax.axis_size("col")
    r = lax.axis_index("row")
    c = lax.axis_index("col")
    local_rows, local_cols = schur.shape
    block_rows, block_cols = local_rows // BLK, local_cols // BLK
    gpr = local_rows // local_cols
    held, kw = panel_raw.shape[0] // BLK, panel_raw.shape[1]
    snw = diag_inverse.shape[0]
    blocks = perm.shape[0]
    bf16 = jnp.bfloat16

    n_pos = n_col // 2
    dma = pltpu.SemaphoreType.DMA
    smem = pl.BlockSpec(memory_space=pltpu.SMEM)
    hbm = pl.BlockSpec(memory_space=pltpu.HBM)
    rows, cols, table = pl.pallas_call(
        functools.partial(general_exchange, n_row, n_col, gpr, held, block_cols, block_rows),
        out_shape=(
            jax.ShapeDtypeStruct((n_col, gpr, BLK, snw), bf16),
            jax.ShapeDtypeStruct((local_cols, snw), bf16),
            jax.ShapeDtypeStruct((block_cols + block_rows,), jnp.int32),
        ),
        in_specs=[smem, hbm, hbm],
        out_specs=(
            pl.BlockSpec(memory_space=pl.ANY),
            pl.BlockSpec(memory_space=pl.ANY),
            smem,
        ),
        scratch_shapes=[
            pltpu.VMEM((held, BLK, kw), bf16),
            pltpu.VMEM((n_col, BLK, kw), bf16),
            pltpu.VMEM((gpr, BLK, snw), bf16),
            pltpu.VMEM((n_col, BLK, kw), bf16),
            pltpu.VMEM((gpr, BLK, snw), bf16),
            pltpu.VMEM((snw, snw), bf16),
            pltpu.VMEM((n_col, BLK, snw), bf16),
            pltpu.VMEM((local_cols, snw), bf16),
            dma((n_row, gpr)), dma((n_row, gpr)), dma((n_col,)), dma((n_col,)),
            dma((n_row,)), dma((n_row,)), dma((n_pos, gpr)), dma((n_pos, gpr)),
            dma((n_pos, gpr)), dma((n_pos, gpr)), dma((n_pos, gpr)), dma((n_pos, gpr)), dma((4,)),
        ],
        compiler_params=pltpu.CompilerParams(
            collective_id=0, has_side_effects=True, vmem_limit_bytes=20 * 2**20
        ),
        cost_estimate=pl.CostEstimate(
            flops=2 * (local_cols + gpr * BLK) * snw * snw,
            bytes_accessed=30 * local_rows * snw,
            transcendentals=0,
        ),
    )(perm, panel_raw.reshape(held, BLK, kw), diag_inverse)

    tile = 4 if block_rows % 4 == 0 else 1

    def row_spec(e):
        return pl.BlockSpec(
            (1, 1, BLK, snw),
            lambda i, t, p: (t[block_cols + tile * i + e], (tile * i + e) // block_cols, 0, 0),
        )

    wide = pl.BlockSpec((tile * BLK, local_cols), lambda i, t, p: (i, 0))
    return pl.pallas_call(
        functools.partial(general_update, tile),
        out_shape=jax.ShapeDtypeStruct(schur.shape, schur.dtype),
        grid_spec=pltpu.PrefetchScalarGridSpec(
            num_scalar_prefetch=2,
            grid=(block_rows // tile,),
            in_specs=[row_spec(e) for e in range(tile)]
            + [pl.BlockSpec((local_cols, snw), lambda i, t, p: (0, 0)), wide],
            out_specs=wide,
        ),
        compiler_params=pltpu.CompilerParams(vmem_limit_bytes=28 * 2**20),
    )(table, pattern.T, *([rows] * tile), cols, schur)


def mix(a, b):
    return 2 * ((a // 2 + b // 2) % 2) + (a % 2 + b % 2) % 2


ROW_PIECES = (
    (1, 2, 3, 4, 5, 6, 7, 8, 9, 10, 11, 12, 13, 14, 15, 16),
    (1, 2, 3, 4, 5, 6, 7, 8, 9, 10, 11, 12, 13, 14, 15, 16),
    (1, 2, 3, 4, 5, 6, 7, 8, 9, 10, 11, 12, 13, 14, 15, 16),
    (1, 2, 3, 4, 5, 6, 7, 8, 9, 10, 11, 12, 13, 14, 15, 16),
    (1, 2, 3, 4, 5, 6, 7, 8, 9, 10, 11, 12, 13, 14, 15, 16),
)
RING_PIECES = (
    (4, 4, 4, 4, 4, 4, 4, 4, 4, 4, 4, 4, 4, 4, 4, 4),
    (4, 4, 4, 4, 4, 4, 4, 4, 4, 4, 4, 4, 4, 4, 4, 4),
    (4, 4, 4, 4, 4, 4, 4, 4, 4, 4, 4, 4, 4, 4, 4, 4),
    (4, 4, 4, 4, 4, 4, 4, 4, 4, 4, 4, 4, 4, 4, 4, 4),
    (4, 4, 4, 4, 4, 4, 4, 4, 4, 4, 4, 4, 4, 4, 4, 4),
)
OWN_PIECES = (
    (0, 0, 0, 2, 4, 6, 6, 6, 6, 7, 8, 8, 8, 8, 8, 8),
    (0, 0, 0, 2, 4, 6, 7, 8, 8, 8, 8, 8, 8, 8, 8, 8),
    (0, 0, 0, 2, 4, 6, 7, 8, 8, 8, 8, 8, 8, 8, 8, 8),
    (0, 0, 0, 2, 4, 6, 7, 8, 8, 8, 8, 8, 8, 8, 8, 8),
    (0, 0, 0, 2, 4, 6, 7, 8, 8, 8, 8, 8, 8, 8, 8, 8),
)
WORK = {
    9: (
        (None, (
            ('rows', 0),
            ('cols', 0),
            ('mul', 0, 0),
        )),
    ),
    11: (
        (0, (
            ('rows', 1),
            ('cols', 1),
            ('mul', 0, 1),
            ('mul', 1, 0),
            ('mul', 1, 1),
        )),
    ),
    12: (
        (0, (
            ('rows', 2),
            ('cols', 2),
            ('mul', 0, 2),
            ('mul', 1, 2),
            ('mul', 2, 0),
            ('mul', 2, 1),
            ('mul', 2, 2),
        )),
        (1, (
            ('rows', 1),
            ('cols', 1),
            ('mul', 0, 1),
            ('mul', 1, 0),
            ('mul', 1, 1),
        )),
    ),
    13: (
        (0, (
            ('cols', 3),
            ('mul', 0, 3),
            ('mul', 1, 3),
            ('mul', 2, 3),
        )),
        (1, (
            ('rows', 2),
            ('cols', 2),
            ('mul', 0, 2),
            ('mul', 1, 2),
            ('mul', 2, 0),
            ('mul', 2, 1),
            ('mul', 2, 2),
        )),
    ),
    14: (
        (0, (
            ('part', 0),
            ('part', 1),
        )),
    ),
    15: (
        (1, (
            ('cols', 3),
            ('mul', 0, 3),
            ('mul', 1, 3),
            ('mul', 2, 3),
            ('part', 0),
            ('part', 1),
        )),
        (None, (
            ('part', 2),
            ('part', 3),
        )),
    ),
}
RING = ()
FAR_STEP = 6


def exchange_kernel(
    held, block_cols, block_rows,
    perm_ref, raw_hbm, d_hbm, u_ref, table_ref,
    raw_ref, sorted_ref, rows_ref, cols_ref, z_ref, d_ref,
    a_send, b_send, z_send, z_recv, s_send, s_recv, c_send, c_recv, loc,
):
    r = lax.axis_index("row")
    c = lax.axis_index("col")
    z = c // 2
    k = c % 2
    sibling = z * 2 + 1 - k
    n_col = sorted_ref.shape[0]
    kw = raw_ref.shape[2]
    snw = d_ref.shape[0]
    inner = ((z + 1) // 2) % 2
    end = 3 * (z // 2)
    diag = (r == z) & (inner == 0)
    order = (z, 1 + z % 2, (2 + 3 * z) % 5, 3 - end)
    rel = mix(r, z)
    load_raw = pltpu.make_async_copy(raw_hbm, raw_ref, loc.at[0])
    load_raw.start()
    load_d = pltpu.make_async_copy(d_hbm, d_ref, loc.at[1])
    load_d.start()

    def remote(src, dst, ssem, rsem, rr, cc):
        return pltpu.make_async_remote_copy(
            src_ref=src, dst_ref=dst, send_sem=ssem, recv_sem=rsem,
            device_id=(rr, cc), device_id_type=MESH,
        )

    def part(index):
        return pl.ds(pl.multiple_of(index * kw, kw), kw)

    barrier = pltpu.get_barrier_semaphore()

    def greet(rr, cc):
        pl.semaphore_signal(barrier, inc=1, device_id=(rr, cc), device_id_type=MESH)

    for rho in (1, 2, 3):
        greet(mix(r, rho), c)
    for rho in (1, 2):
        greet(mix(r, rho), sibling)
    for dc in range(1, n_col):
        greet(r, (c + dc) % n_col)

    groups = [lax.div(perm_ref[c * held + i], block_cols) for i in range(held)]
    load_raw.wait()
    for g in range(n_col):
        block = 0
        for i in range(1, held):
            block = jnp.where(groups[i] == g, i, block)
        sorted_ref[g] = raw_ref[block]
    rows_ref[c, :, :, part(r)] = sorted_ref[pl.ds(r * 2, 2)]
    cols_ref[c, :, part(r)] = sorted_ref[c]
    pl.semaphore_wait(barrier, n_col + 4)

    def pick(index, values):
        found = values[0]
        for n, value in enumerate(values[1:]):
            if any(v != values[0] for v in values[1:]):
                found = jnp.where(index == n + 1, value, found)
        return found

    place = jnp.where(inner == 1, 0, jnp.where(rel == 0, 1, jnp.where(
        rel == 3, 3, jnp.where(rel == 1 + k, 2, 4))))

    def seq(i):
        m = i - 4
        inside = jnp.where(m % 2 == 0, order[1], order[2])
        outside = jnp.where(m < 4, order[1], order[2])
        middle = jnp.where(inner == 1, inside, outside)
        zs = jnp.where(i < 4, z, jnp.where(i < 12, middle, order[3]))
        rho = jnp.where((i >= 4) & (i < 12) & (inner == 1), m // 2, i % 4)
        return zs, rho

    def a_copy(rho):
        other = mix(r, rho)
        return remote(sorted_ref.at[pl.ds(other * 2, 2)], rows_ref.at[c, :, :, part(r)],
                      a_send.at[rho], z_recv.at[z, rho], other, c)

    def piece(zs, rho, core):
        return rows_ref.at[2 * zs + core, :, :, part(mix(r, rho))]

    def z_copy(zs, rho, way):
        ref = piece(zs, rho, k)
        return remote(ref, ref, z_send.at[zs, rho, way], z_recv.at[zs, rho],
                      r, c + 2 - 4 * way)

    def s_copy(zs, rho, core):
        ref = piece(zs, rho, core)
        return remote(ref, ref, s_send.at[zs, rho], s_recv.at[zs, rho], r, sibling)

    def spread(zs, rho, q):
        at = part(mix(r, rho))
        return remote(rows_ref.at[2 * zs + k, q, :, at], cols_ref.at[2 * zs + k, :, at],
                      c_send.at[zs, rho, q], c_recv.at[zs, rho, k],
                      mix(r, 1 + q), z * 2 + q)

    turn = (rel // 2 + rel % 2 + 1 + k) % 2
    onward = mix(r, 2 * (1 - turn) + turn)
    last = (rel // 2 + rel % 2 == 1) & (rel % 2 == k)

    def c_copy(zs, rho, lane):
        ref = cols_ref.at[2 * zs + lane, :, part(mix(z, rho))]
        return remote(ref, ref, c_send.at[zs, rho, lane], c_recv.at[zs, rho, lane], onward, c)

    def direct(zs, rho, lane):
        ref = cols_ref.at[2 * zs + lane, :, part(r)]
        return remote(ref, ref, c_send.at[zs, rho, lane], c_recv.at[zs, rel, lane],
                      mix(r, rho), c)

    def b_copy(zz, kk):
        cc = 2 * zz + kk
        return remote(sorted_ref.at[cc], cols_ref.at[c, :, part(r)],
                      b_send.at[cc], c_recv.at[z, mix(r, zz), k], r, cc)

    def sends_up(zs):
        return (zs <= z) & (z < 3)

    def sends_down(zs):
        return (zs >= z) & (z > 0)

    def forward(zs, rho):
        @pl.when(sends_down(zs))
        def _():
            z_copy(zs, rho, 1).start()

        @pl.when(sends_up(zs))
        def _():
            z_copy(zs, rho, 0).start()

        s_copy(zs, rho, k).start()

    def row_event(i, _):
        zs, rho = seq(i)
        z_copy(zs, rho, 0).wait_recv()
        forward(zs, rho)

        @pl.when(diag & (i >= 4) & (i < 4 + 4 * len(RING)))
        def _():
            for q in range(2):
                spread(zs, rho, q).start()
        return 0

    def ring_event(i, _):
        zs, rho = seq(i)
        for lane in range(2):
            c_copy(zs, rho, lane).wait_recv()

            @pl.when(jnp.logical_not(last))
            def _():
                c_copy(zs, rho, lane).start()
        return 0

    def own_event(b, _):
        b = jnp.where((inner == 0) & (b >= 2), b + 2 * len(RING), b)
        zs = jnp.where(b < 2, z, jnp.where(b < 4, order[1], jnp.where(b < 6, order[2], order[3])))
        lane = (k + b) % 2

        @pl.when(b > 0)
        def _():
            direct(zs, 1, lane).wait_recv()

        for rho in (2, 1, 3):
            direct(zs, rho, lane).start()
        return 0

    def rows_ready(j):
        for rho in range(4):
            s_copy(order[j], rho, 1 - k).wait_recv()

    def blocks(zs):
        return pl.ds(2 * zs, 2)

    def columns(zs):
        return pl.ds(pl.multiple_of(zs * 2 * BLK, 2 * BLK), 2 * BLK)

    def transform(j):
        zs = order[j]

        def arrived():
            for rho in (1, 2, 3):
                for lane in range(2):
                    other = mix(r, rho)
                    ref = cols_ref.at[2 * zs + lane, :, part(other)]
                    remote(ref, ref, c_send.at[zs, rho, lane],
                           c_recv.at[zs, mix(other, z), lane], other, c).wait_recv()

        if j in RING:
            pl.when(inner == 1)(arrived)

            @pl.when(diag)
            def _():
                cols_ref[blocks(zs)] = rows_ref[blocks(zs), k]
        else:
            arrived()

        left = cols_ref[blocks(zs)].reshape(2 * BLK, snw)
        owned = []
        for n in range(0, snw, kw):
            owned.append(
                times_inverse(left[:, : n + kw], d_ref[n : n + kw, : n + kw]).astype(jnp.bfloat16)
            )
        owned = jnp.concatenate(owned, axis=1)
        for n in range(0, snw, kw):
            z_ref[columns(zs), n : n + kw] = lax.dot_general(
                owned[:, n:], d_ref[n:, n : n + kw], (((1,), (0,)), ((), ())),
                preferred_element_type=jnp.float32,
            ).astype(jnp.bfloat16)

    def update(ja, jb):
        za, zb = order[ja], order[jb]
        left = rows_ref[blocks(za)].reshape(4 * BLK, snw)
        at = pl.ds(pl.multiple_of(za * 4 * BLK, 4 * BLK), 4 * BLK)
        u_ref[at, columns(zb)] = times_inverse(left, z_ref[columns(zb), :])

    def last_rows(rho):
        zs = order[3]
        s_copy(zs, rho, 1 - k).wait_recv()
        at = pl.ds(pl.multiple_of(zs * 4 * BLK, 4 * BLK), 4 * BLK)
        deep = part(mix(r, rho))
        left = rows_ref[blocks(zs), :, :, deep].reshape(4 * BLK, kw)
        for b in range(4):
            cols = slice(b * 2 * BLK, (b + 1) * 2 * BLK)
            more = times_inverse(left, z_ref[cols, deep])
            u_ref[at, cols] = more if rho == 0 else u_ref[at, cols] + more

    def do(work):
        for name, *args in work:
            {"rows": rows_ready, "cols": transform, "part": last_rows, "mul": update}[name](*args)

    far_sends = []
    if 1 not in RING:
        far_sends.append((inner == 1, end))
    if 2 not in RING:
        far_sends.append((inner == 1, 3 - end))
    far_sends.append((inner == 0, 3 - z))
    late_sends = [(inner == 0, order[2])]

    def spread_far(sends, wait=False):
        for wanted, zz in sends:
            @pl.when(wanted)
            def _():
                for kk in (k, 1 - k):
                    copy = b_copy(zz, kk)
                    copy.wait_send() if wait else copy.start()

    near_sends = ((z, 1 - k), (order[1], k), (order[1], 1 - k))
    forward(z, 0)
    for rho in (1, 2, 3):
        a_copy(rho).start()
    for zz, kk in near_sends:
        b_copy(zz, kk).start()
    spread_far(far_sends)

    for h in range(perm_ref.shape[0] // held):
        spots = [jnp.int32(0)] * 3
        for b in range(held):
            at = perm_ref[h * held + b]
            group = lax.div(at, block_cols)
            for n, wanted in enumerate((2 * r, 2 * r + 1, c)):
                spots[n] = jnp.where(group == wanted, at, spots[n])
        table_ref[2 * h] = spots[0] - block_rows * r
        table_ref[2 * h + 1] = spots[1] - block_rows * r
        table_ref[16 + h] = spots[2] - block_cols * c

    load_d.wait()
    done = [1, 4, 0]
    for step in range(16):
        events = ((ROW_PIECES, row_event), (RING_PIECES, ring_event), (OWN_PIECES, own_event))
        for n, (counts, event) in enumerate(events):
            upto = pick(place, [line[step] for line in counts])
            lax.fori_loop(done[n], upto, event, 0)
            done[n] = upto
            if n == 0 and step == FAR_STEP:
                spread_far(late_sends)
        for where, work in WORK.get(step, ()):
            if where is None:
                do(work)
            else:
                pl.when(inner == where)(functools.partial(do, work))

    for rho in (1, 2, 3):
        a_copy(rho).wait_send()
    for zz, kk in near_sends:
        b_copy(zz, kk).wait_send()
    spread_far(far_sends, True)
    spread_far(late_sends, True)

    def finish(i, _):
        zs, rho = i // 4, i % 4
        s_copy(zs, rho, k).wait_send()

        @pl.when(sends_up(zs))
        def _():
            z_copy(zs, rho, 0).wait_send()

        @pl.when(sends_down(zs))
        def _():
            z_copy(zs, rho, 1).wait_send()

        plain = inner == 1
        for j in range(4):
            if j not in RING:
                plain = plain | (zs == order[j])
        for lane in range(2):
            @pl.when(plain & (rho > 0))
            def _():
                direct(zs, rho, lane).wait_send()

            @pl.when(jnp.logical_not(plain) & diag)
            def _():
                spread(zs, rho, lane).wait_send()

            @pl.when(jnp.logical_not(plain) & (rel != 0) & jnp.logical_not(last))
            def _():
                c_copy(zs, rho, lane).wait_send()
        return 0

    lax.fori_loop(0, 16, finish, 0)


def finish_kernel(perm_table, pat_ref, u_ref, schur_ref, out_ref, tile_ref, sem):
    slots = tile_ref.shape[0]
    started = [None] * slots
    for j in range(u_ref.shape[0] // BLK):
        slot = j % slots
        if started[slot] is not None:
            started[slot].wait()
        w = perm_table[j]
        rows = pl.ds(pl.multiple_of(w * BLK, BLK), BLK)
        for h in range(u_ref.shape[1] // BLK):
            v = perm_table[16 + h]
            cols = pl.ds(pl.multiple_of(v * BLK, BLK), BLK)
            weight = pat_ref[v, w].astype(jnp.float32)
            tile_ref[slot, :, cols] = (
                schur_ref[rows, cols]
                - u_ref[j * BLK : (j + 1) * BLK, h * BLK : (h + 1) * BLK] * weight
            )
        started[slot] = pltpu.make_async_copy(tile_ref.at[slot], out_ref.at[rows], sem.at[slot])
        started[slot].start()
    for copy in started:
        copy.wait()


def local(schur, panel_raw, diag_inverse, perm, pattern):
    n_row = lax.axis_size("row")
    n_col = lax.axis_size("col")
    local_rows, local_cols = schur.shape
    block_rows, block_cols = local_rows // BLK, local_cols // BLK
    held, kw = panel_raw.shape[0] // BLK, panel_raw.shape[1]
    snw = diag_inverse.shape[0]
    if (n_row, n_col, held, block_rows, block_cols) != (4, 8, 8, 16, 8):
        return general_local(schur, panel_raw, diag_inverse, perm, pattern)
    bf16 = jnp.bfloat16
    dma = pltpu.SemaphoreType.DMA
    smem = pl.BlockSpec(memory_space=pltpu.SMEM)
    vmem = pl.BlockSpec(memory_space=pltpu.VMEM)
    hbm = pl.BlockSpec(memory_space=pl.ANY)

    def stay(x):
        return pltpu.with_memory_space_constraint(x, pltpu.HBM)

    product, table = pl.pallas_call(
        functools.partial(exchange_kernel, held, block_cols, block_rows),
        out_shape=(
            jax.ShapeDtypeStruct((local_rows, local_cols), jnp.float32),
            jax.ShapeDtypeStruct((block_rows + block_cols,), jnp.int32),
        ),
        in_specs=[smem, hbm, hbm],
        out_specs=(vmem, smem),
        scratch_shapes=[
            pltpu.VMEM((held, BLK, kw), bf16),
            pltpu.VMEM((n_col, BLK, kw), bf16),
            pltpu.VMEM((n_col, 2, BLK, snw), bf16),
            pltpu.VMEM((n_col, BLK, snw), bf16),
            pltpu.VMEM((local_cols, snw), bf16),
            pltpu.VMEM((snw, snw), bf16),
            dma((4,)), dma((n_col,)), dma((4, 4, 2)), dma((4, 4)), dma((4, 4)), dma((4, 4)),
            dma((4, 4, 2)), dma((4, 4, 2)), dma((2,)),
        ],
        compiler_params=pltpu.CompilerParams(
            collective_id=0, has_side_effects=True, vmem_limit_bytes=40 * 2**20
        ),
        cost_estimate=pl.CostEstimate(
            flops=2 * 3 * local_rows * local_cols * snw,
            bytes_accessed=30 * local_rows * snw,
            transcendentals=0,
        ),
    )(stay(perm), stay(panel_raw.reshape(held, BLK, kw)), stay(diag_inverse))
    return pl.pallas_call(
        finish_kernel,
        out_shape=jax.ShapeDtypeStruct(schur.shape, schur.dtype),
        in_specs=[smem, smem, vmem, vmem],
        out_specs=hbm,
        scratch_shapes=[pltpu.VMEM((8, BLK, local_cols), jnp.float32), dma((8,))],
        compiler_params=pltpu.CompilerParams(vmem_limit_bytes=8 * 2**20),
    )(table, pattern.T, product, schur)


def solution(mesh):
    return jax.shard_map(
        local,
        mesh=mesh,
        in_specs=(P("row", "col"), P("col", "row"), P(), P(), P("row", "col")),
        out_specs=P("row", "col"),
        check_vma=False,
    )
```

```python
import functools

import jax
import jax.numpy as jnp
from jax import lax
from jax.experimental import pallas as pl
from jax.experimental.pallas import tpu as pltpu
from jax.sharding import PartitionSpec as P

BLK = 128
MESH = pl.DeviceIdType.MESH


def times_inverse(left, right):
    return lax.dot_general(
        left, right, (((1,), (1,)), ((), ())), preferred_element_type=jnp.float32
    )


def general_exchange(
    n_row, n_col, gpr, held, block_cols, block_rows,
    perm_ref, raw_hbm, d_hbm, rows_ref, cols_hbm, table_ref,
    raw_ref, sorted_ref, a_ref, b_ref, own_ref, d_ref, cpan_ref, cols_ref,
    a_send, a_recv, b_send, b_recv, c_send, c_recv,
    up_send, up_recv, down_send, down_recv, f_send, f_recv, loc,
):
    r = lax.axis_index("row")
    c = lax.axis_index("col")
    n_pos = n_col // 2
    pos = c // 2
    core = c % 2
    sibling = pos * 2 + (1 - core)
    kw = raw_ref.shape[2]
    snw = d_ref.shape[0]
    load_raw = pltpu.make_async_copy(raw_hbm, raw_ref, loc.at[3])
    load_raw.start()
    load_d = pltpu.make_async_copy(d_hbm, d_ref, loc.at[0])
    load_d.start()

    def remote(src, dst, ssem, rsem, rr, cc):
        return pltpu.make_async_remote_copy(
            src_ref=src, dst_ref=dst, send_sem=ssem, recv_sem=rsem,
            device_id=(rr, cc), device_id_type=MESH,
        )

    def part(index):
        return pl.ds(pl.multiple_of(index * kw, kw), kw)

    barrier = pltpu.get_barrier_semaphore()
    for dr in range(1, n_row):
        pl.semaphore_signal(barrier, inc=1, device_id=((r + dr) % n_row, c), device_id_type=MESH)
    for dc in range(1, n_col):
        pl.semaphore_signal(barrier, inc=1, device_id=(r, (c + dc) % n_col), device_id_type=MESH)
    groups = [lax.div(perm_ref[c * held + i], block_cols) for i in range(held)]
    load_raw.wait()
    for g in range(n_col):
        block = 0
        for i in range(1, held):
            block = jnp.where(groups[i] == g, i, block)
        sorted_ref[g] = raw_ref[block]
    pl.semaphore_wait(barrier, n_row + n_col - 2)

    def a_copy(dr, q, came=None):
        to = (r + dr) % n_row
        return remote(sorted_ref.at[to * gpr + q],
                      a_ref.at[q, :, part(r if came is None else came)],
                      a_send.at[dr, q], a_recv.at[dr, q], to, c)

    def b_copy(dc, came=None):
        to = (c + dc) % n_col
        return remote(sorted_ref.at[to], b_ref.at[c if came is None else came],
                      b_send.at[dc], b_recv.at[dc], r, to)

    for q in range(gpr):
        for dr in range(1, n_row):
            a_copy(dr, q).start()
    for dc in range(1, n_col):
        b_copy(dc).start()
    a_ref[:, :, part(r)] = sorted_ref[pl.ds(r * gpr, gpr)]
    b_ref[c] = sorted_ref[c]
    load_d.wait()
    def up_copy(d, q):
        slot = (pos - d) * 2 + core
        return remote(own_ref.at[q] if d == 0 else rows_ref.at[slot, q], rows_ref.at[slot, q],
                      up_send.at[d, q], up_recv.at[d, q], r, (pos + 1) * 2 + core)

    def down_copy(d, q):
        slot = (pos + d) * 2 + core
        return remote(own_ref.at[q] if d == 0 else rows_ref.at[slot, q], rows_ref.at[slot, q],
                      down_send.at[d, q], down_recv.at[d, q], r, (pos - 1) * 2 + core)

    def side_copy(source, q, mine):
        slot = source * 2 + core
        return remote(own_ref.at[q] if mine else rows_ref.at[slot, q], rows_ref.at[slot, q],
                      f_send.at[source, q], f_recv.at[source, q], r, sibling)

    for q in range(gpr):
        for dr in range(1, n_row):
            a_copy(dr, q, (r + n_row - dr) % n_row).wait_recv()
        own_ref[q] = times_inverse(a_ref[q], d_ref[...]).astype(jnp.bfloat16)

        @pl.when(pos < n_pos - 1)
        def _(q=q):
            up_copy(0, q).start()

        @pl.when(pos > 0)
        def _(q=q):
            down_copy(0, q).start()

    for q in range(gpr):
        side_copy(pos, q, True).start()
    keep = pltpu.make_async_copy(own_ref, rows_ref.at[c], loc.at[1])
    keep.start()

    for dc in range(1, n_col):
        b_copy(dc, (c + n_col - dc) % n_col).wait_recv()

    def c_copy(dr, came=None):
        return remote(b_ref, cpan_ref.at[:, :, part(r if came is None else came)],
                      c_send.at[dr], c_recv.at[dr], (r + dr) % n_row, c)

    for dr in range(1, n_row):
        c_copy(dr).start()
    cpan_ref[:, :, part(r)] = b_ref[...]

    wanted = [c * block_cols + k for k in range(block_cols)]
    wanted += [r * block_rows + k for k in range(block_rows)]

    def look(p, found):
        at, holder = perm_ref[p], p // held
        return tuple(jnp.where(at == w, holder, f) for w, f in zip(wanted, found))

    holders = lax.fori_loop(
        0, perm_ref.shape[0], look, tuple(jnp.int32(0) for _ in wanted)
    )
    for k, value in enumerate(holders):
        table_ref[k] = value

    keep_cols = pltpu.make_async_copy(cols_ref, cols_hbm, loc.at[2])

    def factor_columns():
        for dr in range(1, n_row):
            c_copy(dr, (r + n_row - dr) % n_row).wait_recv()
        step = 4 if block_cols % 4 == 0 else 1
        for w in range(0, block_cols, step):
            left = jnp.concatenate([cpan_ref[holders[w + k]] for k in range(step)], axis=0)
            done = times_inverse(left, d_ref[...]).astype(jnp.bfloat16)
            cols_ref[w * BLK:(w + step) * BLK, :] = done
        keep_cols.start()

    for d in range(1, n_pos):
        if d == n_pos - 1:
            factor_columns()

        for q in range(gpr):
            @pl.when(pos - d >= 0)
            def _(d=d, q=q):
                slot = (pos - d) * 2 + core
                remote(own_ref.at[q], rows_ref.at[slot, q], up_send.at[d - 1, q],
                       up_recv.at[d - 1, q], r, sibling).wait_recv()
                if d < n_pos - 1:
                    @pl.when(pos < n_pos - 1)
                    def _():
                        up_copy(d, q).start()
                side_copy(pos - d, q, False).start()

            @pl.when(pos + d <= n_pos - 1)
            def _(d=d, q=q):
                slot = (pos + d) * 2 + core
                remote(own_ref.at[q], rows_ref.at[slot, q], down_send.at[d - 1, q],
                       down_recv.at[d - 1, q], r, sibling).wait_recv()
                if d < n_pos - 1:
                    @pl.when(pos > 0)
                    def _():
                        down_copy(d, q).start()
                side_copy(pos + d, q, False).start()

    for dr in range(1, n_row):
        for q in range(gpr):
            a_copy(dr, q).wait_send()
        c_copy(dr).wait_send()
    for dc in range(1, n_col):
        b_copy(dc).wait_send()
    for q in range(gpr):
        for d in range(n_pos - 1):
            @pl.when((pos - d >= 0) & (pos < n_pos - 1))
            def _(d=d, q=q):
                up_copy(d, q).wait_send()

            @pl.when((pos + d <= n_pos - 1) & (pos > 0))
            def _(d=d, q=q):
                down_copy(d, q).wait_send()
        for source in range(n_pos):
            slot = source * 2 + (1 - core)
            remote(own_ref.at[q], rows_ref.at[slot, q], f_send.at[source, q],
                   f_recv.at[source, q], r, sibling).wait_recv()
            side_copy(source, q, True).wait_send()
    keep.wait()
    keep_cols.wait()


def general_update(tile, table, pat_ref, *refs):
    row_refs, (cols_ref, schur_ref, out_ref) = refs[:tile], refs[tile:]
    i = pl.program_id(0)
    left = jnp.concatenate([ref[0, 0] for ref in row_refs], axis=0)
    update = times_inverse(left, cols_ref[...])
    for e in range(tile):
        rows = slice(e * BLK, (e + 1) * BLK)
        for w in range(cols_ref.shape[0] // BLK):
            at = slice(w * BLK, (w + 1) * BLK)
            weight = pat_ref[w, tile * i + e].astype(jnp.float32)
            out_ref[rows, at] = schur_ref[rows, at] - update[rows, at] * weight


def general_local(schur, panel_raw, diag_inverse, perm, pattern):
    n_row = lax.axis_size("row")
    n_col = lax.axis_size("col")
    r = lax.axis_index("row")
    c = lax.axis_index("col")
    local_rows, local_cols = schur.shape
    block_rows, block_cols = local_rows // BLK, local_cols // BLK
    gpr = local_rows // local_cols
    held, kw = panel_raw.shape[0] // BLK, panel_raw.shape[1]
    snw = diag_inverse.shape[0]
    blocks = perm.shape[0]
    bf16 = jnp.bfloat16

    n_pos = n_col // 2
    dma = pltpu.SemaphoreType.DMA
    smem = pl.BlockSpec(memory_space=pltpu.SMEM)
    hbm = pl.BlockSpec(memory_space=pltpu.HBM)
    rows, cols, table = pl.pallas_call(
        functools.partial(general_exchange, n_row, n_col, gpr, held, block_cols, block_rows),
        out_shape=(
            jax.ShapeDtypeStruct((n_col, gpr, BLK, snw), bf16),
            jax.ShapeDtypeStruct((local_cols, snw), bf16),
            jax.ShapeDtypeStruct((block_cols + block_rows,), jnp.int32),
        ),
        in_specs=[smem, hbm, hbm],
        out_specs=(
            pl.BlockSpec(memory_space=pl.ANY),
            pl.BlockSpec(memory_space=pl.ANY),
            smem,
        ),
        scratch_shapes=[
            pltpu.VMEM((held, BLK, kw), bf16),
            pltpu.VMEM((n_col, BLK, kw), bf16),
            pltpu.VMEM((gpr, BLK, snw), bf16),
            pltpu.VMEM((n_col, BLK, kw), bf16),
            pltpu.VMEM((gpr, BLK, snw), bf16),
            pltpu.VMEM((snw, snw), bf16),
            pltpu.VMEM((n_col, BLK, snw), bf16),
            pltpu.VMEM((local_cols, snw), bf16),
            dma((n_row, gpr)), dma((n_row, gpr)), dma((n_col,)), dma((n_col,)),
            dma((n_row,)), dma((n_row,)), dma((n_pos, gpr)), dma((n_pos, gpr)),
            dma((n_pos, gpr)), dma((n_pos, gpr)), dma((n_pos, gpr)), dma((n_pos, gpr)), dma((4,)),
        ],
        compiler_params=pltpu.CompilerParams(
            collective_id=0, has_side_effects=True, vmem_limit_bytes=20 * 2**20
        ),
        cost_estimate=pl.CostEstimate(
            flops=2 * (local_cols + gpr * BLK) * snw * snw,
            bytes_accessed=30 * local_rows * snw,
            transcendentals=0,
        ),
    )(perm, panel_raw.reshape(held, BLK, kw), diag_inverse)

    tile = 4 if block_rows % 4 == 0 else 1

    def row_spec(e):
        return pl.BlockSpec(
            (1, 1, BLK, snw),
            lambda i, t, p: (t[block_cols + tile * i + e], (tile * i + e) // block_cols, 0, 0),
        )

    wide = pl.BlockSpec((tile * BLK, local_cols), lambda i, t, p: (i, 0))
    return pl.pallas_call(
        functools.partial(general_update, tile),
        out_shape=jax.ShapeDtypeStruct(schur.shape, schur.dtype),
        grid_spec=pltpu.PrefetchScalarGridSpec(
            num_scalar_prefetch=2,
            grid=(block_rows // tile,),
            in_specs=[row_spec(e) for e in range(tile)]
            + [pl.BlockSpec((local_cols, snw), lambda i, t, p: (0, 0)), wide],
            out_specs=wide,
        ),
        compiler_params=pltpu.CompilerParams(vmem_limit_bytes=28 * 2**20),
    )(table, pattern.T, *([rows] * tile), cols, schur)


def mix(a, b):
    return 2 * ((a // 2 + b // 2) % 2) + (a % 2 + b % 2) % 2


ROW_PIECES = (
    (1, 2, 3, 4, 5, 6, 7, 8, 9, 10, 11, 12, 13, 14, 15, 16, 16),
    (1, 2, 3, 4, 5, 6, 7, 8, 9, 10, 11, 12, 12, 12, 12, 14, 16),
    (1, 2, 3, 4, 5, 6, 7, 8, 9, 10, 11, 12, 12, 12, 12, 14, 16),
    (1, 2, 3, 4, 5, 6, 7, 8, 9, 10, 11, 12, 12, 12, 12, 14, 16),
    (1, 2, 3, 4, 5, 6, 7, 8, 9, 10, 11, 12, 12, 12, 12, 14, 16),
)
RING_PIECES = (
    (4, 4, 4, 4, 4, 4, 4, 4, 4, 4, 4, 4, 4, 4, 4, 4, 4),
    (4, 4, 4, 4, 4, 4, 4, 4, 4, 4, 4, 4, 4, 4, 4, 4, 4),
    (4, 4, 4, 4, 4, 4, 4, 4, 4, 4, 4, 4, 4, 4, 4, 4, 4),
    (4, 4, 4, 4, 4, 4, 4, 4, 4, 4, 4, 4, 4, 4, 4, 4, 4),
    (4, 4, 4, 4, 4, 4, 4, 4, 4, 4, 4, 4, 4, 4, 4, 4, 4),
)
OWN_PIECES = (
    (0, 0, 0, 2, 4, 4, 6, 6, 6, 7, 8, 8, 8, 8, 8, 8, 8),
    (0, 0, 0, 2, 3, 4, 5, 7, 8, 8, 8, 8, 8, 8, 8, 8, 8),
    (0, 0, 0, 2, 3, 4, 5, 7, 8, 8, 8, 8, 8, 8, 8, 8, 8),
    (0, 0, 0, 2, 3, 4, 5, 7, 8, 8, 8, 8, 8, 8, 8, 8, 8),
    (0, 0, 0, 2, 3, 4, 5, 7, 8, 8, 8, 8, 8, 8, 8, 8, 8),
)
WORK = {
    7: (
        (0, (
            ('cols', 0),
        )),
    ),
    8: (
        (0, (
            ('rows', 0),
            ('rows', 1),
            ('mul', 0, 0),
            ('mul', 1, 0),
        )),
    ),
    9: (
        (1, (
            ('rows', 0),
            ('cols', 0),
            ('mul', 0, 0),
        )),
    ),
    11: (
        (0, (
            ('cols', 1),
            ('mul', 0, 1),
            ('mul', 1, 1),
        )),
    ),
    12: (
        (0, (
            ('rows', 2),
            ('mul', 2, 0),
            ('mul', 2, 1),
        )),
        (1, (
            ('rows', 1),
            ('cols', 1),
            ('mul', 0, 1),
            ('mul', 1, 0),
            ('mul', 1, 1),
        )),
    ),
    13: (
        (0, (
            ('cols', 2),
            ('mul', 0, 2),
            ('mul', 1, 2),
            ('mul', 2, 2),
        )),
        (1, (
            ('rows', 2),
            ('cols', 2),
            ('mul', 0, 2),
            ('mul', 1, 2),
            ('mul', 2, 0),
            ('mul', 2, 1),
            ('mul', 2, 2),
        )),
    ),
    14: (
        (0, (
            ('cols', 3),
            ('mul', 0, 3),
            ('mul', 1, 3),
            ('mul', 2, 3),
        )),
    ),
    15: (
        (0, (
            ('part', 0, 0, 1, 2, 3),
            ('part', 1, 0, 1, 2, 3),
        )),
        (1, (
            ('cols', 3),
            ('mul', 0, 3),
            ('mul', 1, 3),
            ('mul', 2, 3),
            ('part', 0, 0, 1, 2, 3),
            ('part', 1, 0, 1, 2, 3),
            ('part', 2, 0, 1, 2, 3),
            ('part', 3, 0, 1, 2, 3),
        )),
    ),
    16: (
        (0, (
            ('part', 2, 0, 1, 2, 3),
            ('part', 3, 0, 1, 2, 3),
        )),
    ),
}
RING = ()
FAR_STEP = 6


def exchange_kernel(
    held, block_cols, block_rows,
    perm_hbm, raw_hbm, d_hbm, u_ref, table_ref,
    perm_ref, raw_ref, sorted_ref, rows_ref, cols_ref, z_ref, d_ref,
    a_send, b_send, z_send, z_recv, s_send, s_recv, c_send, c_recv, loc,
):
    r = lax.axis_index("row")
    c = lax.axis_index("col")
    z = c // 2
    k = c % 2
    sibling = z * 2 + 1 - k
    n_col = sorted_ref.shape[0]
    kw = raw_ref.shape[2]
    snw = d_ref.shape[0]
    inner = ((z + 1) // 2) % 2
    end = 3 * (z // 2)
    diag = (r == z) & (inner == 0)
    order = (z, 1 + z % 2, (2 + 3 * z) % 5, 3 - end)
    rel = mix(r, z)
    load_perm = pltpu.make_async_copy(perm_hbm, perm_ref, loc.at[2])
    load_perm.start()
    load_raw = pltpu.make_async_copy(raw_hbm, raw_ref, loc.at[0])
    load_raw.start()
    load_d = pltpu.make_async_copy(d_hbm, d_ref, loc.at[1])
    load_d.start()

    def remote(src, dst, ssem, rsem, rr, cc):
        return pltpu.make_async_remote_copy(
            src_ref=src, dst_ref=dst, send_sem=ssem, recv_sem=rsem,
            device_id=(rr, cc), device_id_type=MESH,
        )

    def part(index):
        return pl.ds(pl.multiple_of(index * kw, kw), kw)

    barrier = pltpu.get_barrier_semaphore()

    def greet(rr, cc):
        pl.semaphore_signal(barrier, inc=1, device_id=(rr, cc), device_id_type=MESH)

    for rho in (1, 2, 3):
        greet(mix(r, rho), c)
    for rho in (1, 2):
        greet(mix(r, rho), sibling)
    for dc in range(1, n_col):
        greet(r, (c + dc) % n_col)

    load_perm.wait()
    groups = [lax.div(perm_ref[c * held + i], block_cols) for i in range(held)]
    load_raw.wait()
    def sort(g):
        block = 0
        for i in range(1, held):
            block = jnp.where(groups[i] == g, i, block)
        return raw_ref[block]

    for q in range(2):
        rows_ref[c, q, :, part(r)] = sort(2 * r + q)
    pl.semaphore_wait(barrier, n_col + 4)

    def pick(index, values):
        found = values[0]
        for n, value in enumerate(values[1:]):
            if any(v != values[0] for v in values[1:]):
                found = jnp.where(index == n + 1, value, found)
        return found

    place = jnp.where(inner == 1, 0, jnp.where(rel == 0, 1, jnp.where(
        rel == 3, 3, jnp.where(rel == 1 + k, 2, 4))))

    def seq(i):
        m = i - 4
        inside = jnp.where(m % 2 == 0, order[1], order[2])
        outside = jnp.where(m < 4, order[1], order[2])
        middle = jnp.where(inner == 1, inside, outside)
        zs = jnp.where(i < 4, z, jnp.where(i < 12, middle, order[3]))
        rho = jnp.where((i >= 4) & (i < 12) & (inner == 1), m // 2, i % 4)
        return zs, rho

    def a_copy(rho):
        other = mix(r, rho)
        return remote(sorted_ref.at[pl.ds(other * 2, 2)], rows_ref.at[c, :, :, part(r)],
                      a_send.at[rho], z_recv.at[z, rho], other, c)

    def piece(zs, rho, core):
        return rows_ref.at[2 * zs + core, :, :, part(mix(r, rho))]

    def z_copy(zs, rho, way):
        ref = piece(zs, rho, k)
        return remote(ref, ref, z_send.at[zs, rho, way], z_recv.at[zs, rho],
                      r, c + 2 - 4 * way)

    def s_copy(zs, rho, core):
        ref = piece(zs, rho, core)
        return remote(ref, ref, s_send.at[zs, rho], s_recv.at[zs, rho], r, sibling)

    def spread(zs, rho, q):
        at = part(mix(r, rho))
        return remote(rows_ref.at[2 * zs + k, q, :, at], cols_ref.at[2 * zs + k, :, at],
                      c_send.at[zs, rho, q], c_recv.at[zs, rho, k],
                      mix(r, 1 + q), z * 2 + q)

    turn = (rel // 2 + rel % 2 + 1 + k) % 2
    onward = mix(r, 2 * (1 - turn) + turn)
    last = (rel // 2 + rel % 2 == 1) & (rel % 2 == k)

    def c_copy(zs, rho, lane):
        ref = cols_ref.at[2 * zs + lane, :, part(mix(z, rho))]
        return remote(ref, ref, c_send.at[zs, rho, lane], c_recv.at[zs, rho, lane], onward, c)

    def direct(zs, rho, lane):
        ref = cols_ref.at[2 * zs + lane, :, part(r)]
        return remote(ref, ref, c_send.at[zs, rho, lane], c_recv.at[zs, rel, lane],
                      mix(r, rho), c)

    def b_copy(zz, kk):
        cc = 2 * zz + kk
        return remote(sorted_ref.at[cc], cols_ref.at[c, :, part(r)],
                      b_send.at[cc], c_recv.at[z, mix(r, zz), k], r, cc)

    def sends_up(zs):
        return (zs <= z) & (z < 3)

    def sends_down(zs):
        return (zs >= z) & (z > 0)

    def forward(zs, rho):
        @pl.when(sends_down(zs))
        def _():
            z_copy(zs, rho, 1).start()

        @pl.when(sends_up(zs))
        def _():
            z_copy(zs, rho, 0).start()

        s_copy(zs, rho, k).start()

    def row_event(i, _):
        zs, rho = seq(i)
        z_copy(zs, rho, 0).wait_recv()
        forward(zs, rho)

        @pl.when(diag & (i >= 4) & (i < 4 + 4 * len(RING)))
        def _():
            for q in range(2):
                spread(zs, rho, q).start()
        return 0

    def ring_event(i, _):
        zs, rho = seq(i)
        for lane in range(2):
            c_copy(zs, rho, lane).wait_recv()

            @pl.when(jnp.logical_not(last))
            def _():
                c_copy(zs, rho, lane).start()
        return 0

    def own_event(b, _):
        b = jnp.where((inner == 0) & (b >= 2), b + 2 * len(RING), b)
        zs = jnp.where(b < 2, z, jnp.where(b < 4, order[1], jnp.where(b < 6, order[2], order[3])))
        lane = (k + b) % 2

        @pl.when(b > 0)
        def _():
            direct(zs, 1, lane).wait_recv()

        for rho in (2, 1, 3):
            direct(zs, rho, lane).start()
        return 0

    def rows_ready(j):
        for rho in range(4):
            s_copy(order[j], rho, 1 - k).wait_recv()

    def blocks(zs):
        return pl.ds(2 * zs, 2)

    def columns(zs):
        return pl.ds(pl.multiple_of(zs * 2 * BLK, 2 * BLK), 2 * BLK)

    def transform(j):
        zs = order[j]

        def arrived():
            for rho in (1, 2, 3):
                for lane in range(2):
                    other = mix(r, rho)
                    ref = cols_ref.at[2 * zs + lane, :, part(other)]
                    remote(ref, ref, c_send.at[zs, rho, lane],
                           c_recv.at[zs, mix(other, z), lane], other, c).wait_recv()

        if j in RING:
            pl.when(inner == 1)(arrived)

            @pl.when(diag)
            def _():
                cols_ref[blocks(zs)] = rows_ref[blocks(zs), k]
        else:
            arrived()

        left = cols_ref[blocks(zs)].reshape(2 * BLK, snw)
        owned = []
        for n in range(0, snw, kw):
            owned.append(
                times_inverse(left[:, : n + kw], d_ref[n : n + kw, : n + kw]).astype(jnp.bfloat16)
            )
        owned = jnp.concatenate(owned, axis=1)
        for n in range(0, snw, kw):
            z_ref[columns(zs), n : n + kw] = lax.dot_general(
                owned[:, n:], d_ref[n:, n : n + kw], (((1,), (0,)), ((), ())),
                preferred_element_type=jnp.float32,
            ).astype(jnp.bfloat16)

    def update(ja, jb):
        za, zb = order[ja], order[jb]
        left = rows_ref[blocks(za)].reshape(4 * BLK, snw)
        at = pl.ds(pl.multiple_of(za * 4 * BLK, 4 * BLK), 4 * BLK)
        u_ref[at, columns(zb)] = times_inverse(left, z_ref[columns(zb), :])

    def last_rows(rho, *groups):
        zs = order[3]
        s_copy(zs, rho, 1 - k).wait_recv()
        at = pl.ds(pl.multiple_of(zs * 4 * BLK, 4 * BLK), 4 * BLK)
        deep = part(mix(r, rho))
        left = rows_ref[blocks(zs), :, :, deep].reshape(4 * BLK, kw)
        for jb in groups:
            cols = columns(order[jb])
            more = times_inverse(left, z_ref[cols, deep])
            u_ref[at, cols] = more if rho == 0 else u_ref[at, cols] + more

    def do(work):
        for name, *args in work:
            {"rows": rows_ready, "cols": transform, "part": last_rows, "mul": update}[name](*args)

    far_sends = []
    if 1 not in RING:
        far_sends.append((inner == 1, end))
    if 2 not in RING:
        far_sends.append((inner == 1, 3 - end))
    far_sends.append((inner == 0, 3 - z))
    late_sends = [(inner == 0, order[2])]

    def spread_far(sends, wait=False):
        for wanted, zz in sends:
            @pl.when(wanted)
            def _():
                for kk in (k, 1 - k):
                    copy = b_copy(zz, kk)
                    copy.wait_send() if wait else copy.start()

    near_sends = ((z, 1 - k), (order[1], k), (order[1], 1 - k))
    forward(z, 0)
    for g in range(n_col):
        sorted_ref[g] = sort(g)
    for rho in (1, 2, 3):
        a_copy(rho).start()
    cols_ref[c, :, part(r)] = sorted_ref[c]
    for zz, kk in near_sends:
        b_copy(zz, kk).start()
    spread_far(far_sends)

    for h in range(perm_ref.shape[0] // held):
        spots = [jnp.int32(0)] * 3
        for b in range(held):
            at = perm_ref[h * held + b]
            group = lax.div(at, block_cols)
            for n, wanted in enumerate((2 * r, 2 * r + 1, c)):
                spots[n] = jnp.where(group == wanted, at, spots[n])
        table_ref[2 * h] = spots[0] - block_rows * r
        table_ref[2 * h + 1] = spots[1] - block_rows * r
        table_ref[16 + h] = spots[2] - block_cols * c

    load_d.wait()
    done = [1, 4, 0]
    for step in range(len(ROW_PIECES[0])):
        events = ((ROW_PIECES, row_event), (RING_PIECES, ring_event), (OWN_PIECES, own_event))
        for n, (counts, event) in enumerate(events):
            upto = pick(place, [line[step] for line in counts])
            lax.fori_loop(done[n], upto, event, 0)
            done[n] = upto
            if n == 0 and step == FAR_STEP:
                spread_far(late_sends)
        for where, work in WORK.get(step, ()):
            if where is None:
                do(work)
            else:
                pl.when(inner == where)(functools.partial(do, work))

    for rho in (1, 2, 3):
        a_copy(rho).wait_send()
    for zz, kk in near_sends:
        b_copy(zz, kk).wait_send()
    spread_far(far_sends, True)
    spread_far(late_sends, True)

    def finish(i, _):
        zs, rho = i // 4, i % 4
        s_copy(zs, rho, k).wait_send()

        @pl.when(sends_up(zs))
        def _():
            z_copy(zs, rho, 0).wait_send()

        @pl.when(sends_down(zs))
        def _():
            z_copy(zs, rho, 1).wait_send()

        plain = inner == 1
        for j in range(4):
            if j not in RING:
                plain = plain | (zs == order[j])
        for lane in range(2):
            @pl.when(plain & (rho > 0))
            def _():
                direct(zs, rho, lane).wait_send()

            @pl.when(jnp.logical_not(plain) & diag)
            def _():
                spread(zs, rho, lane).wait_send()

            @pl.when(jnp.logical_not(plain) & (rel != 0) & jnp.logical_not(last))
            def _():
                c_copy(zs, rho, lane).wait_send()
        return 0

    lax.fori_loop(0, 16, finish, 0)


def finish_kernel(perm_table, pat_ref, u_ref, schur_ref, out_ref, tile_ref, sem):
    slots = tile_ref.shape[0]
    started = [None] * slots
    for j in range(u_ref.shape[0] // BLK):
        slot = j % slots
        if started[slot] is not None:
            started[slot].wait()
        w = perm_table[j]
        rows = pl.ds(pl.multiple_of(w * BLK, BLK), BLK)
        for h in range(u_ref.shape[1] // BLK):
            v = perm_table[16 + h]
            cols = pl.ds(pl.multiple_of(v * BLK, BLK), BLK)
            weight = pat_ref[v, w].astype(jnp.float32)
            tile_ref[slot, :, cols] = (
                schur_ref[rows, cols]
                - u_ref[j * BLK : (j + 1) * BLK, h * BLK : (h + 1) * BLK] * weight
            )
        started[slot] = pltpu.make_async_copy(tile_ref.at[slot], out_ref.at[rows], sem.at[slot])
        started[slot].start()
    for copy in started:
        copy.wait()


def local(schur, panel_raw, diag_inverse, perm, pattern):
    n_row = lax.axis_size("row")
    n_col = lax.axis_size("col")
    local_rows, local_cols = schur.shape
    block_rows, block_cols = local_rows // BLK, local_cols // BLK
    held, kw = panel_raw.shape[0] // BLK, panel_raw.shape[1]
    snw = diag_inverse.shape[0]
    if (n_row, n_col, held, block_rows, block_cols) != (4, 8, 8, 16, 8):
        return general_local(schur, panel_raw, diag_inverse, perm, pattern)
    bf16 = jnp.bfloat16
    dma = pltpu.SemaphoreType.DMA
    smem = pl.BlockSpec(memory_space=pltpu.SMEM)
    vmem = pl.BlockSpec(memory_space=pltpu.VMEM)
    hbm = pl.BlockSpec(memory_space=pl.ANY)

    def stay(x):
        return pltpu.with_memory_space_constraint(x, pltpu.HBM)

    product, table = pl.pallas_call(
        functools.partial(exchange_kernel, held, block_cols, block_rows),
        out_shape=(
            jax.ShapeDtypeStruct((local_rows, local_cols), jnp.float32),
            jax.ShapeDtypeStruct((block_rows + block_cols,), jnp.int32),
        ),
        in_specs=[hbm, hbm, hbm],
        out_specs=(vmem, smem),
        scratch_shapes=[
            pltpu.SMEM(perm.shape, jnp.int32),
            pltpu.VMEM((held, BLK, kw), bf16),
            pltpu.VMEM((n_col, BLK, kw), bf16),
            pltpu.VMEM((n_col, 2, BLK, snw), bf16),
            pltpu.VMEM((n_col, BLK, snw), bf16),
            pltpu.VMEM((local_cols, snw), bf16),
            pltpu.VMEM((snw, snw), bf16),
            dma((4,)), dma((n_col,)), dma((4, 4, 2)), dma((4, 4)), dma((4, 4)), dma((4, 4)),
            dma((4, 4, 2)), dma((4, 4, 2)), dma((3,)),
        ],
        compiler_params=pltpu.CompilerParams(
            collective_id=0, has_side_effects=True, vmem_limit_bytes=40 * 2**20
        ),
        cost_estimate=pl.CostEstimate(
            flops=2 * 3 * local_rows * local_cols * snw,
            bytes_accessed=30 * local_rows * snw,
            transcendentals=0,
        ),
    )(stay(perm), stay(panel_raw.reshape(held, BLK, kw)), stay(diag_inverse))
    return pl.pallas_call(
        finish_kernel,
        out_shape=jax.ShapeDtypeStruct(schur.shape, schur.dtype),
        in_specs=[smem, smem, vmem, vmem],
        out_specs=hbm,
        scratch_shapes=[pltpu.VMEM((8, BLK, local_cols), jnp.float32), dma((8,))],
        compiler_params=pltpu.CompilerParams(vmem_limit_bytes=8 * 2**20),
    )(table, pattern.T, product, schur)


def solution(mesh):
    return jax.shard_map(
        local,
        mesh=mesh,
        in_specs=(P("row", "col"), P("col", "row"), P(), P(), P("row", "col")),
        out_specs=P("row", "col"),
        check_vma=False,
    )
```
